32 devices in a mesh: seq: 8 (over z, x), head: 4 (over y, core).
Axes of the slice: x: 2, y: 2, z: 4, core: 2. Of those that a mesh axis runs over, the one named last changes fastest.
Arguments:
- hidden_in: bfloat16 [8192, 2048], P('seq', 'head'), may hold values from -6 to 6
- value_weight: bfloat16 [2048, 2048], P(None, 'head'), may hold values from -0.125 to 0.125
- queries: bfloat16 [8192, 2048], P('seq', 'head'), may hold values from -6 to 6
- keys: bfloat16 [8192, 2048], P('seq', 'head'), may hold values from -6 to 6
- level_weights: bfloat16 [14, 16, 8192], P(None, 'head', 'seq'), may hold values from 0 to 1
- out_grad: bfloat16 [8192, 2048], P('seq', 'head'), may hold values from -0.0625 to 0.0625
Outputs:
- attended: bfloat16 [8192, 2048], P('seq', 'head')
- weight_grad: float32 [2048, 2048], P('seq', 'head')
The draws below stay inside these ranges and needn't reach their ends.
All inputs are finite; a program needn't handle non-finite values.
Results may differ from the reference program's by a relative error of at most 0.0057.
Values may be sent and summed in bfloat16 or wider, within the bound.
A program may use at most 128 MiB of HBM per device.

```python
import math
import jax
import jax.numpy as jnp
from jax import lax

D = 2048
H = 16
HD = 128
TOK_DEV = 1024
TOKENS = 8192
TOK_BITS = 10
SEQ_BITS = 3
LEVELS = 14
N_SEQ = 8


def draw_level_weights(key, part):
    level_axis = jnp.arange(LEVELS, dtype=jnp.float32)[:, None, None]
    spread = jnp.exp2(jnp.maximum(level_axis - 1.0, 0.0))
    base = jnp.exp(jax.random.uniform(key, (LEVELS, H, TOKENS), jnp.float32, math.log(0.1), math.log(2.0)))
    return (base / jnp.sqrt(HD * spread)).astype(jnp.bfloat16)


def strengthened(entries, stream_key, source, target, parts, factor):
    def block_of(dim):
        return (jnp.arange(entries.shape[dim]) // (entries.shape[dim] // parts)).reshape((-1,) + (1,) * (entries.ndim - 1 - dim))

    first = jax.random.permutation(stream_key, parts)[block_of(target)]
    far = (block_of(target) + parts // 2) % parts
    return jnp.where((block_of(source) == first) | (block_of(source) == far), factor * entries, entries)


def block_levels(own_key, dims, cuts, smallest, largest):
    level, own = 1.0, jax.random.fold_in(own_key, 6)
    for dim, blocks in cuts:
        steps = jnp.exp(jax.random.uniform(jax.random.fold_in(own, dim), (blocks,), jnp.float32, smallest / len(cuts), largest / len(cuts)))
        level = level * jnp.repeat(steps, dims[dim] // blocks).reshape([-1 if axis == dim else 1 for axis in range(len(dims))])
    return level


def normal_values(rng, shape, deviation, reach, cuts=(), kind=jnp.bfloat16):
    entries = deviation * jax.random.normal(rng, shape, jnp.float32)
    if cuts:
        entries = entries * block_levels(rng, shape, cuts, -0.22, 0.18)
    return jnp.clip(entries, -reach, reach).astype(kind)


def gaussian_with(stream_key, dims, scale, limit, cuts, heavy, kind=jnp.bfloat16):
    entries = scale * jax.random.normal(stream_key, dims, jnp.float32)
    if cuts:
        entries = entries * block_levels(stream_key, dims, cuts, -0.22, 0.18)
    return jnp.clip(strengthened(entries, jax.random.fold_in(stream_key, 3), *heavy), -limit, limit).astype(kind)


def setup_inputs(seed: int = 0) -> dict:
    seeds = jax.random.split(jax.random.key(seed), 7)
    return {
        "hidden_in": gaussian_with(seeds[0], (TOKENS, D), 1.0, 6.0, ((0, 8), (1, 4)), (0, 1, 8, 2.0)),
        "value_weight": normal_values(seeds[1], (D, H * HD), D ** -0.5, 0.125, ((1, 4),)),
        "queries": normal_values(seeds[2], (TOKENS, H * HD), 1.0, 6.0, ((0, 8), (1, 4))),
        "keys": normal_values(seeds[3], (TOKENS, H * HD), 1.0, 6.0, ((0, 8), (1, 4))),
        "level_weights": draw_level_weights(jax.random.fold_in(seeds[6], 71), 0),
        "out_grad": normal_values(seeds[5], (TOKENS, H * HD), (TOKENS ** -0.5), 0.0625, ((0, 8), (1, 4))),
    }


def rounded_copy(array):
    return lax.optimization_barrier(array.astype(jnp.bfloat16)).astype(jnp.float32)


def level_of(later, earlier, depth):
    differ = jnp.bitwise_xor(later, earlier)
    result = jnp.zeros(differ.shape, jnp.int32)
    for digit in range(depth):
        result = result + (differ >= (1 << digit)).astype(jnp.int32)
    return result


def near_block(queries3, keys3, values3, grads3, near_weights, depth):
    length = queries3.shape[0]
    count = max(1, length // 512)
    span_rows = length // count
    pieces = []
    value_back = jnp.zeros(values3.shape, jnp.float32)
    for index in range(count):
        first = index * span_rows
        last = first + span_rows
        scores = jnp.einsum("thd,shd->hts", queries3[first:last].astype(jnp.float32),
                            keys3[:last].astype(jnp.float32), precision=lax.Precision.HIGHEST)
        later = first + jnp.arange(span_rows, dtype=jnp.int32)[:, None]
        earlier = jnp.arange(last, dtype=jnp.int32)[None, :]
        table = level_of(later, earlier, depth)
        weight = jnp.zeros(scores.shape, jnp.float32)
        for level_index in range(depth + 1):
            weight = weight + jnp.where(table == level_index, near_weights[level_index][:, first:last, None], 0.0)
        weight = jnp.where(earlier <= later, weight, 0.0)
        probs = rounded_copy(scores * weight)
        pieces.append(jnp.einsum("hts,she->the", probs, values3[:last].astype(jnp.float32),
                                 precision=lax.Precision.HIGHEST))
        value_back = value_back.at[:last].add(jnp.einsum("hts,the->she", probs, grads3[first:last].astype(jnp.float32),
                                                         precision=lax.Precision.HIGHEST))
    return jnp.concatenate(pieces, axis=0), value_back


def reference(hidden_in, value_weight, queries, keys, level_weights, out_grad):
    head_count = level_weights.shape[1]
    span_cols = value_weight.shape[1]
    head_width = span_cols // head_count
    values = jnp.dot(hidden_in, value_weight, preferred_element_type=jnp.float32).astype(jnp.bfloat16)
    shape_four = (N_SEQ, TOK_DEV, head_count, head_width)
    queries4 = queries.reshape(shape_four)
    keys4 = keys.reshape(shape_four)
    values4 = values.reshape(shape_four)
    grads4 = out_grad.reshape(shape_four)
    near_weights = level_weights[:TOK_BITS + 1].astype(jnp.float32).reshape(
        TOK_BITS + 1, head_count, N_SEQ, TOK_DEV).transpose(2, 0, 1, 3)
    far_weights = level_weights[TOK_BITS + 1:].astype(jnp.float32).reshape(
        SEQ_BITS, head_count, N_SEQ, TOK_DEV)

    def one_block(packed):
        return near_block(packed[0], packed[1], packed[2], packed[3], packed[4], TOK_BITS)

    attended, value_grad = lax.map(one_block, (queries4, keys4, values4, grads4, near_weights))
    queries_wide = queries4.astype(jnp.float32)
    keys_wide = keys4.astype(jnp.float32)
    key_state = jnp.einsum("bthd,bthe->bhde", keys_wide, values4.astype(jnp.float32),
                           precision=lax.Precision.HIGHEST)
    block_index = jnp.arange(N_SEQ, dtype=jnp.int32)
    for digit in range(SEQ_BITS):
        group_size = 1 << digit
        group_count = N_SEQ // group_size
        group_of = block_index >> digit
        upper = (group_of & 1) == 1
        grouped = key_state.reshape(group_count, group_size, head_count, head_width, head_width).sum(axis=1)
        chosen = grouped[jnp.maximum(group_of - 1, 0)]
        far_state = jnp.where(upper[:, None, None, None], chosen, 0.0)
        level_scale = far_weights[digit].transpose(1, 2, 0)[:, :, :, None]
        product = jnp.einsum("bthd,bhde->bthe", queries_wide, rounded_copy(far_state),
                             precision=lax.Precision.HIGHEST)
        attended = attended + product * level_scale
        weighted = rounded_copy(queries_wide * level_scale)
        query_state = jnp.einsum("bthd,bthe->bhde", weighted, grads4.astype(jnp.float32),
                                 precision=lax.Precision.HIGHEST)
        grouped_back = query_state.reshape(group_count, group_size, head_count, head_width, head_width).sum(axis=1)
        chosen_back = grouped_back[jnp.minimum(group_of + 1, group_count - 1)]
        back_state = jnp.where(upper[:, None, None, None], 0.0, chosen_back)
        value_grad = value_grad + jnp.einsum("bshd,bhde->bshe", keys_wide, rounded_copy(back_state),
                                             precision=lax.Precision.HIGHEST)
    attended_out = attended.astype(jnp.bfloat16).reshape(TOKENS, span_cols)
    value_flat = value_grad.astype(jnp.bfloat16).reshape(TOKENS, span_cols)
    weight_grad = lax.dot_general(hidden_in, value_flat, (((0,), (0,)), ((), ())),
                                  preferred_element_type=jnp.float32)
    return attended_out, weight_grad
```

```python
import functools

import jax
import jax.numpy as jnp
from jax import lax
from jax.experimental import pallas as pl
from jax.experimental.pallas import tpu as pltpu
from jax.sharding import PartitionSpec as P

MESH = pl.DeviceIdType.MESH
F32 = jnp.float32
BF16 = jnp.bfloat16
SUB = 128
TILE = 256
CHUNKS = 4


def bits_of(n):
    return n.bit_length() - 1


def digit_of(index, digit):
    return lax.rem(lax.div(index, 1 << digit), 2)


def flip(index, digit):
    return index + (1 << digit) - (2 << digit) * digit_of(index, digit)


def xor_bit(a, b):
    return a + b - 2 * a * b


def dot(a, b):
    return jnp.dot(a, b, preferred_element_type=F32)


def kernel(cfg, hid, vw, q, k, lw, g, att_out, wg_out,
           gath, vw_v, q_v, k_v, g_v, lw_v, lwf, wqt, near, vb, vg, vals, attt,
           att_v, qs, qacc, qsend, qrecv, krun, ksend, krecv, wgf, wg_v, *rest):
    nh, n, heads, hd, T, C = cfg
    hb, sb = bits_of(nh), bits_of(n)
    kb = sb - hb
    wsend, wrecv = rest[:kb], rest[kb:2 * kb]
    osend, orecv = rest[2 * kb:2 * kb + hb], rest[2 * kb + hb:2 * kb + 2 * hb]
    (lsem, gss, grs, qss, qrs, kss, krs, wss, wrs, oss, ors, outsem) = rest[2 * kb + 2 * hb:]
    depth = bits_of(T)
    subbits = bits_of(SUB)
    h = lax.axis_index("head")
    b = lax.axis_index("seq")

    locals_ = [pltpu.make_async_copy(s, d, lsem.at[i]) for i, (s, d) in enumerate(
        [(q, q_v), (lw, lw_v), (g, g_v), (k, k_v), (hid, gath.at[0]), (vw, vw_v)])]
    for c in locals_:
        c.start()
    barrier = pltpu.get_barrier_semaphore()
    for i in range(hb):
        pl.semaphore_signal(barrier, inc=1, device_id={"head": flip(h, i)}, device_id_type=MESH)
    for i in range(sb):
        pl.semaphore_signal(barrier, inc=1, device_id={"seq": flip(b, i)}, device_id_type=MESH)
    pl.semaphore_wait(barrier, hb + sb)

    rows = T // CHUNKS

    def gcopy(slot, bit, c):
        src = hid if slot == 0 else gath.at[slot]
        part = pl.ds(c * rows, rows)
        return pltpu.make_async_remote_copy(
            src_ref=src.at[part], dst_ref=gath.at[slot | (1 << bit), part],
            send_sem=gss.at[slot | (1 << bit), c], recv_sem=grs.at[slot | (1 << bit), c],
            device_id={"head": flip(h, bit)}, device_id_type=MESH)

    def low(slot):
        return bits_of(slot & -slot)

    copies = []

    def go(copy):
        copy.start()
        copies.append(copy)
        return copy

    inflight = {}

    def gstart(slot, bit, c):
        inflight[slot | (1 << bit), c] = go(gcopy(slot, bit, c))

    for bit in reversed(range(hb)):
        for c in range(CHUNKS):
            gstart(0, bit, c)

    arrived = set()

    def need(slot, c):
        if slot == 0 or (slot, c) in arrived:
            return
        arrived.add((slot, c))
        inflight[slot, c].wait_recv()
        for bit in range(low(slot)):
            gstart(slot, bit, c)

    def forward(c):
        for slot in range(nh - 1, 0, -1):
            if low(slot) > 0:
                need(slot, c)

    def cols(i):
        return pl.ds(i * hd, hd)

    for i in range(3):
        locals_[i].wait()
    lwf[...] = lw_v[...].astype(F32)
    for i in range(heads):
        qt = q_v[:, cols(i)].astype(F32).T
        gi = g_v[:, cols(i)]
        for j in range(sb):
            w = (qt * lwf[depth + 1 + j, i:i + 1, :]).astype(BF16)
            wqt[i, pl.ds(j * hd, hd), :] = w
            qs[j, i] = dot(w, gi)

    qcopies = {}

    def qstart(j):
        own = qs[j] * digit_of(b, j).astype(F32)
        value = own if j == sb - 1 else qacc[...] + own
        qsend[j] = value.astype(BF16)
        qcopies[j] = go(pltpu.make_async_remote_copy(
            src_ref=qsend.at[j], dst_ref=qrecv.at[j], send_sem=qss.at[j], recv_sem=qrs.at[j],
            device_id={"seq": flip(b, j)}, device_id_type=MESH))

    def qfinish(j):
        qcopies[j].wait_recv()
        got = qrecv[j].astype(F32)
        qacc[...] = got if j == sb - 1 else qacc[...] + got

    qstart(sb - 1)
    locals_[3].wait()

    later = lax.broadcasted_iota(jnp.int32, (SUB, SUB), 1)
    earlier = lax.broadcasted_iota(jnp.int32, (SUB, SUB), 0)
    differ = jnp.bitwise_xor(later, earlier)
    causal = earlier <= later

    def near_head(i):
        qt = q_v[:, cols(i)].astype(F32).T.astype(BF16)
        for m in range(T // TILE):
            top = (m + 1) * TILE
            s = dot(k_v[:top, cols(i)], qt[:, m * TILE:top])
            for u in range(TILE // SUB):
                ti = m * (TILE // SUB) + u
                tl = slice(ti * SUB, ti * SUB + SUB)
                for si in range(top // SUB):
                    part = s[si * SUB:si * SUB + SUB, u * SUB:u * SUB + SUB]
                    if si > ti:
                        out = jnp.zeros((SUB, SUB), BF16)
                    elif si < ti:
                        level = subbits + (si ^ ti).bit_length()
                        out = (part * lwf[level, i:i + 1, tl]).astype(BF16)
                    else:
                        w = jnp.broadcast_to(lwf[0, i:i + 1, tl], (SUB, SUB))
                        for level in range(subbits):
                            w = jnp.where(differ >= 1 << level, lwf[level + 1, i:i + 1, tl], w)
                        out = (part * jnp.where(causal, w, 0.0)).astype(BF16)
                    near[i, si * SUB:si * SUB + SUB, tl] = out
            back = dot(near[i, :top, m * TILE:top], g_v[m * TILE:top, cols(i)])
            if m == 0:
                vb[:top, cols(i)] = back
            else:
                prev = m * TILE
                vb[:prev, cols(i)] += back[:prev]
                vb[prev:top, cols(i)] = back[prev:]

    jobs = [functools.partial(near_head, i) for i in range(heads)]
    passed = 0
    for index, j in enumerate(reversed(range(sb))):
        take = max(1, heads - (sb - 1)) if index == 0 else 1
        for _ in range(take):
            if jobs:
                jobs.pop(0)()
        if passed < CHUNKS - 1:
            forward(passed)
            passed += 1
        qfinish(j)
        if j > 0:
            qstart(j - 1)
    for job in jobs:
        job()
    for i in range(heads):
        state = qacc[i].astype(BF16)
        vg[:, cols(i)] = (vb[:, cols(i)] + dot(k_v[:, cols(i)], state)).astype(BF16)

    wrows = wgf.shape[1]
    wcopies = {}

    def inner_offset(stage):
        off = 0
        for st in range(stage):
            off = off + digit_of(b, kb - 1 - st) * (wrows >> (st + 1))
        return off

    def wstart(o, st):
        size = wrows >> (st + 1)
        dg = kb - 1 - st
        start = inner_offset(st) + (1 - digit_of(b, dg)) * size
        wsend[st][o] = wgf[o, pl.ds(pl.multiple_of(start, size), size), :].astype(BF16)
        wcopies[o, st] = go(pltpu.make_async_remote_copy(
            src_ref=wsend[st].at[o], dst_ref=wrecv[st].at[o], send_sem=wss.at[o, st],
            recv_sem=wrs.at[o, st], device_id={"seq": flip(b, dg)}, device_id_type=MESH))

    def wfinish(o, st):
        size = wrows >> (st + 1)
        part = pl.ds(pl.multiple_of(inner_offset(st + 1), size), size)
        wcopies[o, st].wait_recv()
        wgf[o, part, :] += wrecv[st][o].astype(F32)

    def wgrad(o):
        for c in range(CHUNKS):
            need(o, c)
        if o == 0:
            pass
        half = wrows // 2
        for r in range(2):
            wgf[o, r * half:(r + 1) * half, :] = lax.dot_general(
                gath[o, :, r * half:(r + 1) * half], vg[...], (((0,), (0,)), ((), ())),
                preferred_element_type=F32)
        if kb:
            wstart(o, 0)

    out_rows = wg_v.shape[0]
    match = [xor_bit(digit_of(h, m), digit_of(b, kb + m)) for m in range(hb)]

    def final_part():
        return pl.ds(pl.multiple_of(inner_offset(kb), out_rows), out_rows)

    def chosen(m, r, keep):
        index = r * (2 << m)
        for i in range(m):
            index = index + match[i] * (1 << i)
        return index + (match[m] if keep else 1 - match[m]) * (1 << m)

    ocopies = {}

    def ostart(m, r):
        osend[m][r] = wgf[chosen(m, r, False), final_part(), :].astype(BF16)
        ocopies[m, r] = go(pltpu.make_async_remote_copy(
            src_ref=osend[m].at[r], dst_ref=orecv[m].at[r], send_sem=oss.at[m, r],
            recv_sem=ors.at[m, r], device_id={"seq": flip(b, kb + m)}, device_id_type=MESH))

    def ofinish(m, r):
        ocopies[m, r].wait_recv()
        wgf[chosen(m, r, True), final_part(), :] += orecv[m][r].astype(F32)

    def inner(o):
        for st in range(kb):
            wfinish(o, st)
            if st + 1 < kb:
                wstart(o, st + 1)

    locals_[4].wait()
    for o in range(nh // 2):
        wgrad(o)
    for c in range(CHUNKS):
        forward(c)

    locals_[5].wait()
    for c in range(CHUNKS):
        for o in range(1, nh):
            need(o, c)
        part = slice(c * rows, (c + 1) * rows)
        total = None
        for o in range(nh):
            source = h
            for bit in range(hb):
                if o >> bit & 1:
                    source = flip(source, bit)
            term = dot(gath[o, part, :], vw_v[pl.ds(pl.multiple_of(source * C, C), C), :])
            total = term if total is None else total + term
        for i in range(heads):
            vals[i, :, part] = total[:, i * hd:(i + 1) * hd].T.astype(BF16)
    for i in range(heads):
        krun[i] = dot(vals[i], k_v[:, cols(i)])

    kcopies = {}

    def kstart(j):
        ksend[j] = krun[...].astype(BF16)
        kcopies[j] = go(pltpu.make_async_remote_copy(
            src_ref=ksend.at[j], dst_ref=krecv.at[j], send_sem=kss.at[j], recv_sem=krs.at[j],
            device_id={"seq": flip(b, j)}, device_id_type=MESH))

    def kfinish(j):
        kcopies[j].wait_recv()
        if j + 1 < sb:
            krun[...] += krecv[j].astype(F32)

    kstart(0)
    for o in range(nh // 2, nh):
        wgrad(o)
    kfinish(0)
    if sb > 1:
        kstart(1)

    def att_near(i):
        for m in range(T // TILE):
            top = (m + 1) * TILE
            attt[i, :, m * TILE:top] = dot(vals[i, :, :top], near[i, :top, m * TILE:top])

    for o in range(nh // 2):
        inner(o)
    for r in range(nh // 4):
        ostart(0, r)
    for i in range(heads // 2):
        att_near(i)
    for j in range(1, sb):
        kfinish(j)
        if j + 1 < sb:
            kstart(j + 1)
        if j == 1:
            for o in range(nh // 2, nh):
                inner(o)
            for r in range(nh // 4, nh // 2):
                ostart(0, r)
            for i in range(heads // 2, heads):
                att_near(i)
    for m in range(hb):
        for r in range(nh >> (m + 1)):
            ofinish(m, r)
        if m + 1 < hb:
            for r in range(nh >> (m + 2)):
                ostart(m + 1, r)
        if m == 0:
            for i in range(heads):
                total = attt[i]
                for j in range(sb):
                    far = (krecv[j, i].astype(F32) * digit_of(b, j).astype(F32)).astype(BF16)
                    total = total + dot(far, wqt[i, pl.ds(j * hd, hd), :])
                att_v[:, cols(i)] = total.T.astype(BF16)
            att_copy = pltpu.make_async_copy(att_v, att_out, outsem.at[0])
            att_copy.start()
    index = 0
    for m in range(hb):
        index = index + match[m] * (1 << m)
    wg_v[...] = wgf[index, final_part(), :]
    wg_copy = pltpu.make_async_copy(wg_v, wg_out, outsem.at[1])
    wg_copy.start()
    for copy in copies:
        copy.wait_send()
    att_copy.wait()
    wg_copy.wait()


def local(hidden_in, value_weight, queries, keys, level_weights, out_grad):
    levels, heads, T = level_weights.shape
    D, C = value_weight.shape
    hd = C // heads
    n, nh = lax.axis_size("seq"), lax.axis_size("head")
    hb, sb = bits_of(nh), bits_of(n)
    kb = sb - hb
    wrows = hidden_in.shape[1]
    out_rows = D // n
    vmem, dma = pltpu.VMEM, pltpu.SemaphoreType.DMA
    state = (heads, hd, hd)
    scratch = [
        vmem((nh, T, wrows), BF16), vmem((D, C), BF16), vmem((T, C), BF16), vmem((T, C), BF16),
        vmem((T, C), BF16), vmem(level_weights.shape, BF16), vmem(level_weights.shape, F32),
        vmem((heads, sb * hd, T), BF16), vmem((heads, T, T), BF16), vmem((T, C), F32),
        vmem((T, C), BF16), vmem((heads, hd, T), BF16), vmem((heads, hd, T), F32),
        vmem((T, C), BF16),
        vmem((sb,) + state, F32), vmem(state, F32), vmem((sb,) + state, BF16),
        vmem((sb,) + state, BF16),
        vmem(state, F32), vmem((sb,) + state, BF16), vmem((sb,) + state, BF16),
        vmem((nh, wrows, C), F32), vmem((out_rows, C), F32),
    ]
    scratch += [vmem((nh, wrows >> (s + 1), C), BF16) for s in range(kb)] * 2
    scratch += [vmem((nh >> (m + 1), out_rows, C), BF16) for m in range(hb)] * 2
    scratch += [
        dma((6,)), dma((nh, CHUNKS)), dma((nh, CHUNKS)), dma((sb,)), dma((sb,)), dma((sb,)),
        dma((sb,)), dma((nh, max(kb, 1))), dma((nh, max(kb, 1))), dma((hb, max(nh // 2, 1))),
        dma((hb, max(nh // 2, 1))), dma((2,)),
    ]
    anyspec = pl.BlockSpec(memory_space=pl.ANY)
    return pl.pallas_call(
        functools.partial(kernel, (nh, n, heads, hd, T, C)),
        out_shape=(jax.ShapeDtypeStruct((T, C), BF16), jax.ShapeDtypeStruct((out_rows, C), F32)),
        in_specs=[anyspec] * 6,
        out_specs=(anyspec, anyspec),
        scratch_shapes=scratch,
        compiler_params=pltpu.CompilerParams(
            collective_id=0, has_side_effects=True, vmem_limit_bytes=60 * 2 ** 20),
    )(hidden_in, value_weight, queries, keys, level_weights, out_grad)


def solution(mesh):
    return jax.shard_map(
        local,
        mesh=mesh,
        in_specs=(
            P("seq", "head"),
            P(None, "head"),
            P("seq", "head"),
            P("seq", "head"),
            P(None, "head", "seq"),
            P("seq", "head"),
        ),
        out_specs=(P("seq", "head"), P("seq", "head")),
        check_vma=False,
    )
```

```python
import functools

import jax
import jax.numpy as jnp
from jax import lax
from jax.experimental import pallas as pl
from jax.experimental.pallas import tpu as pltpu
from jax.sharding import PartitionSpec as P

MESH = pl.DeviceIdType.MESH
F32 = jnp.float32
BF16 = jnp.bfloat16
SUB = 128
TILE = 256
CHUNKS = 2
PARTS = 4


def bits_of(n):
    return n.bit_length() - 1


def digit_of(index, digit):
    return lax.rem(lax.div(index, 1 << digit), 2)


def flip(index, digit):
    return index + (1 << digit) - (2 << digit) * digit_of(index, digit)


def xor_bit(a, b):
    return a + b - 2 * a * b


def dot(a, b):
    return jnp.dot(a, b, preferred_element_type=F32)


def kernel(cfg, hid, vw, q, k, lw, g, att_out, wg_out,
           gath, vw_v, q_v, k_v, g_v, lw_v, lwf, wqt, near, vb, vg, vals, attt,
           att_v, qs, qacc, qsend, qrecv, krun, ksend, krecv, wgf, wg_v, *rest):
    nh, n, heads, hd, T, C = cfg
    hb, sb = bits_of(nh), bits_of(n)
    kb = sb - hb
    wsend, wrecv = rest[:kb], rest[kb:2 * kb]
    osend, orecv = rest[2 * kb:2 * kb + hb], rest[2 * kb + hb:2 * kb + 2 * hb]
    (lsem, gss, grs, qss, qrs, kss, krs, wss, wrs, oss, ors, outsem) = rest[2 * kb + 2 * hb:]
    depth = bits_of(T)
    subbits = bits_of(SUB)
    h = lax.axis_index("head")
    b = lax.axis_index("seq")

    locals_ = [pltpu.make_async_copy(s, d, lsem.at[i]) for i, (s, d) in enumerate(
        [(q, q_v), (lw, lw_v), (g, g_v), (k, k_v), (hid, gath.at[0]), (vw, vw_v)])]
    for c in locals_:
        c.start()
    barrier = pltpu.get_barrier_semaphore()
    for i in range(hb):
        pl.semaphore_signal(barrier, inc=1, device_id={"head": flip(h, i)}, device_id_type=MESH)
    for i in range(sb):
        pl.semaphore_signal(barrier, inc=1, device_id={"seq": flip(b, i)}, device_id_type=MESH)
    pl.semaphore_wait(barrier, hb + sb)

    half = gath.shape[2] // CHUNKS
    first = 1 - digit_of(b, kb - 1)

    def half_of(c):
        return pl.ds(pl.multiple_of((first if c == 0 else 1 - first) * half, half), half)

    def gcopy(slot, bit, c):
        src = hid if slot == 0 else gath.at[slot]
        part = half_of(c)
        return pltpu.make_async_remote_copy(
            src_ref=src.at[:, part], dst_ref=gath.at[slot | (1 << bit), :, part],
            send_sem=gss.at[slot | (1 << bit), c], recv_sem=grs.at[slot | (1 << bit), c],
            device_id={"head": flip(h, bit)}, device_id_type=MESH)

    def low(slot):
        return bits_of(slot & -slot)

    copies = []

    def go(copy):
        copy.start()
        copies.append(copy)
        return copy

    inflight = {}

    def gstart(slot, bit, c):
        inflight[slot | (1 << bit), c] = go(gcopy(slot, bit, c))

    for bit in reversed(range(hb)):
        for c in range(CHUNKS):
            gstart(0, bit, c)

    arrived = set()

    def need(slot, c):
        if slot == 0 or (slot, c) in arrived:
            return
        arrived.add((slot, c))
        inflight[slot, c].wait_recv()
        for bit in range(low(slot)):
            gstart(slot, bit, c)

    def forward(c):
        for slot in range(nh - 1, 0, -1):
            if low(slot) > 0:
                need(slot, c)

    def cols(i):
        return pl.ds(i * hd, hd)

    for i in range(3):
        locals_[i].wait()
    lwf[...] = lw_v[...].astype(F32)
    for i in range(heads):
        qt = q_v[:, cols(i)].astype(F32).T
        gi = g_v[:, cols(i)]
        for j in range(sb):
            w = (qt * lwf[depth + 1 + j, i:i + 1, :]).astype(BF16)
            wqt[i, pl.ds(j * hd, hd), :] = w
            qs[j, i] = dot(w, gi)

    qcopies = {}

    def qstart(j):
        own = qs[j] * digit_of(b, j).astype(F32)
        value = own if j == sb - 1 else qacc[...] + own
        qsend[j] = value.astype(BF16)
        qcopies[j] = go(pltpu.make_async_remote_copy(
            src_ref=qsend.at[j], dst_ref=qrecv.at[j], send_sem=qss.at[j], recv_sem=qrs.at[j],
            device_id={"seq": flip(b, j)}, device_id_type=MESH))

    def qfinish(j):
        qcopies[j].wait_recv()
        got = qrecv[j].astype(F32)
        qacc[...] = got if j == sb - 1 else qacc[...] + got

    qstart(sb - 1)
    locals_[3].wait()

    later = lax.broadcasted_iota(jnp.int32, (SUB, SUB), 1)
    earlier = lax.broadcasted_iota(jnp.int32, (SUB, SUB), 0)
    differ = jnp.bitwise_xor(later, earlier)
    causal = earlier <= later

    def near_head(i):
        qt = q_v[:, cols(i)].astype(F32).T.astype(BF16)
        for m in range(T // TILE):
            top = (m + 1) * TILE
            s = dot(k_v[:top, cols(i)], qt[:, m * TILE:top])
            for u in range(TILE // SUB):
                ti = m * (TILE // SUB) + u
                tl = slice(ti * SUB, ti * SUB + SUB)
                for si in range(top // SUB):
                    part = s[si * SUB:si * SUB + SUB, u * SUB:u * SUB + SUB]
                    if si > ti:
                        out = jnp.zeros((SUB, SUB), BF16)
                    elif si < ti:
                        level = subbits + (si ^ ti).bit_length()
                        out = (part * lwf[level, i:i + 1, tl]).astype(BF16)
                    else:
                        w = jnp.broadcast_to(lwf[0, i:i + 1, tl], (SUB, SUB))
                        for level in range(subbits):
                            w = jnp.where(differ >= 1 << level, lwf[level + 1, i:i + 1, tl], w)
                        out = (part * jnp.where(causal, w, 0.0)).astype(BF16)
                    near[i, si * SUB:si * SUB + SUB, tl] = out
            back = dot(near[i, :top, m * TILE:top], g_v[m * TILE:top, cols(i)])
            if m == 0:
                vb[:top, cols(i)] = back
            else:
                prev = m * TILE
                vb[:prev, cols(i)] += back[:prev]
                vb[prev:top, cols(i)] = back[prev:]

    jobs = [functools.partial(near_head, i) for i in range(heads)]
    for index, j in enumerate(reversed(range(sb))):
        take = max(1, heads - (sb - 1)) if index == 0 else 1
        for _ in range(take):
            if jobs:
                jobs.pop(0)()
        qfinish(j)
        if j > 0:
            qstart(j - 1)
    for job in jobs:
        job()
    forward(0)
    for i in range(heads):
        state = qacc[i].astype(BF16)
        vg[:, cols(i)] = (vb[:, cols(i)] + dot(k_v[:, cols(i)], state)).astype(BF16)

    width = C // PARTS
    wcopies = {}

    def inner_offset(stage):
        off = 0
        for st in range(1, stage):
            off = off + digit_of(b, kb - 1 - st) * (half >> st)
        return off

    def wgo(o, st, cc):
        wcopies[o, st, cc] = go(pltpu.make_async_remote_copy(
            src_ref=wsend[st].at[o, cc], dst_ref=wrecv[st].at[o, cc], send_sem=wss.at[o, st, cc],
            recv_sem=wrs.at[o, st, cc], device_id={"seq": flip(b, kb - 1 - st)},
            device_id_type=MESH))

    def wstart(o, st, cc):
        size = half >> st
        start = inner_offset(st) + (1 - digit_of(b, kb - 1 - st)) * size
        wsend[st][o, cc] = wgf[o, cc, pl.ds(pl.multiple_of(start, size), size), :].astype(BF16)
        wgo(o, st, cc)

    def wfinish(o, st, cc):
        size = half >> st
        part = pl.ds(pl.multiple_of(inner_offset(st + 1), size), size)
        wcopies[o, st, cc].wait_recv()
        wgf[o, cc, part, :] += wrecv[st][o, cc].astype(F32)

    def wgrad(o, c):
        need(o, c)
        rows_t = gath[o, :, half_of(c)]
        for cc in range(PARTS):
            if cc % 2 == 0:
                two = lax.dot_general(rows_t, vg[:, cc * width:(cc + 2) * width],
                                      (((0,), (0,)), ((), ())), preferred_element_type=F32)
            part = two[:, (cc % 2) * width:(cc % 2 + 1) * width]
            if c == 0:
                wsend[0][o, cc] = part.astype(BF16)
            else:
                wgf[o, cc] = part

    out_rows = wg_v.shape[0]
    match = [xor_bit(digit_of(h, m), digit_of(b, kb + m)) for m in range(hb)]

    def final_part():
        return pl.ds(pl.multiple_of(inner_offset(kb), out_rows), out_rows)

    def chosen(m, r, keep):
        index = r * (2 << m)
        for i in range(m):
            index = index + match[i] * (1 << i)
        return index + (match[m] if keep else 1 - match[m]) * (1 << m)

    ocopies = {}

    def ostart(m, cc):
        for r in range(nh >> (m + 1)):
            osend[m][r, cc] = wgf[chosen(m, r, False), cc, final_part(), :].astype(BF16)
            ocopies[m, r, cc] = go(pltpu.make_async_remote_copy(
                src_ref=osend[m].at[r, cc], dst_ref=orecv[m].at[r, cc],
                send_sem=oss.at[m, r, cc], recv_sem=ors.at[m, r, cc],
                device_id={"seq": flip(b, kb + m)}, device_id_type=MESH))

    def ofinish(m, cc):
        for r in range(nh >> (m + 1)):
            ocopies[m, r, cc].wait_recv()
            wgf[chosen(m, r, True), cc, final_part(), :] += orecv[m][r, cc].astype(F32)
        if m + 1 < hb:
            ostart(m + 1, cc)

    def inner(cc):
        for o in range(nh):
            for st in range(kb):
                wfinish(o, st, cc)
                if st + 1 < kb:
                    wstart(o, st + 1, cc)
        ostart(0, cc)

    locals_[4].wait()
    for o in range(nh):
        wgrad(o, 0)
        wgo(o, 0, 0)
    for cc in range(1, PARTS - 1):
        for o in range(nh):
            wgo(o, 0, cc)
    wgrad(0, 1)

    locals_[5].wait()

    def values_part(c):
        for t in range(T // TILE):
            part = slice(t * TILE, (t + 1) * TILE)
            total = None if c == 0 else vb[part, :]
            for o in range(nh):
                source = h
                for bit in range(hb):
                    if o >> bit & 1:
                        source = flip(source, bit)
                start = source * gath.shape[2] + (first if c == 0 else 1 - first) * half
                term = dot(gath[o, part, half_of(c)],
                           vw_v[pl.ds(pl.multiple_of(start, half), half), :])
                total = term if total is None else total + term
            if c + 1 < CHUNKS:
                vb[part, :] = total
            else:
                for i in range(heads):
                    vals[i, :, part] = total[:, i * hd:(i + 1) * hd].T.astype(BF16)

    values_part(0)
    forward(1)
    for o in range(1, nh):
        wgrad(o, 1)
    values_part(1)
    for i in range(heads):
        krun[i] = dot(vals[i], k_v[:, cols(i)])

    kcopies = {}

    def kstart(j):
        ksend[j] = krun[...].astype(BF16)
        kcopies[j] = go(pltpu.make_async_remote_copy(
            src_ref=ksend.at[j], dst_ref=krecv.at[j], send_sem=kss.at[j], recv_sem=krs.at[j],
            device_id={"seq": flip(b, j)}, device_id_type=MESH))

    def kfinish(j):
        kcopies[j].wait_recv()
        if j + 1 < sb:
            krun[...] += krecv[j].astype(F32)
            kstart(j + 1)

    def att_near(i):
        for m in range(T // TILE):
            top = (m + 1) * TILE
            attt[i, :, m * TILE:top] = dot(vals[i, :, :top], near[i, :top, m * TILE:top])

    kstart(0)
    for o in range(nh):
        wgo(o, 0, PARTS - 1)
    jobs = [functools.partial(att_near, i) for i in range(heads)]
    keyed = 0
    for cc in range(PARTS):
        inner(cc)
        if cc > 0:
            ofinish(0, cc - 1)
        if cc + 2 >= PARTS:
            kfinish(keyed)
            keyed += 1
        if jobs:
            jobs.pop(0)()
    for job in jobs:
        job()
    ofinish(0, PARTS - 1)
    while keyed < sb:
        kfinish(keyed)
        keyed += 1
    for i in range(heads):
        total = attt[i]
        for j in range(sb):
            far = (krecv[j, i].astype(F32) * digit_of(b, j).astype(F32)).astype(BF16)
            total = total + dot(far, wqt[i, pl.ds(j * hd, hd), :])
        att_v[:, cols(i)] = total.T.astype(BF16)
    att_copy = pltpu.make_async_copy(att_v, att_out, outsem.at[0])
    att_copy.start()
    for m in range(1, hb):
        for cc in range(PARTS):
            ofinish(m, cc)
    index = 0
    for m in range(hb):
        index = index + match[m] * (1 << m)
    for cc in range(PARTS):
        wg_v[:, cc * width:(cc + 1) * width] = wgf[index, cc, final_part(), :]
    wg_copy = pltpu.make_async_copy(wg_v, wg_out, outsem.at[1])
    wg_copy.start()
    for copy in copies:
        copy.wait_send()
    att_copy.wait()
    wg_copy.wait()


def local(hidden_in, value_weight, queries, keys, level_weights, out_grad):
    levels, heads, T = level_weights.shape
    D, C = value_weight.shape
    hd = C // heads
    n, nh = lax.axis_size("seq"), lax.axis_size("head")
    hb, sb = bits_of(nh), bits_of(n)
    kb = sb - hb
    wrows = hidden_in.shape[1]
    out_rows = D // n
    vmem, dma = pltpu.VMEM, pltpu.SemaphoreType.DMA
    state = (heads, hd, hd)
    scratch = [
        vmem((nh, T, wrows), BF16), vmem((D, C), BF16), vmem((T, C), BF16), vmem((T, C), BF16),
        vmem((T, C), BF16), vmem(level_weights.shape, BF16), vmem(level_weights.shape, F32),
        vmem((heads, sb * hd, T), BF16), vmem((heads, T, T), BF16), vmem((T, C), F32),
        vmem((T, C), BF16), vmem((heads, hd, T), BF16), vmem((heads, hd, T), F32),
        vmem((T, C), BF16),
        vmem((sb,) + state, F32), vmem(state, F32), vmem((sb,) + state, BF16),
        vmem((sb,) + state, BF16),
        vmem(state, F32), vmem((sb,) + state, BF16), vmem((sb,) + state, BF16),
        vmem((nh, PARTS, wrows // 2, C // PARTS), F32), vmem((out_rows, C), F32),
    ]
    scratch += [vmem((nh, PARTS, wrows >> (s + 1), C // PARTS), BF16) for s in range(kb)] * 2
    scratch += [vmem((nh >> (m + 1), PARTS, out_rows, C // PARTS), BF16) for m in range(hb)] * 2
    scratch += [
        dma((6,)), dma((nh, CHUNKS)), dma((nh, CHUNKS)), dma((sb,)), dma((sb,)), dma((sb,)),
        dma((sb,)), dma((nh, kb, PARTS)), dma((nh, kb, PARTS)), dma((hb, nh // 2, PARTS)),
        dma((hb, nh // 2, PARTS)), dma((2,)),
    ]
    anyspec = pl.BlockSpec(memory_space=pl.ANY)
    return pl.pallas_call(
        functools.partial(kernel, (nh, n, heads, hd, T, C)),
        out_shape=(jax.ShapeDtypeStruct((T, C), BF16), jax.ShapeDtypeStruct((out_rows, C), F32)),
        in_specs=[anyspec] * 6,
        out_specs=(anyspec, anyspec),
        scratch_shapes=scratch,
        compiler_params=pltpu.CompilerParams(
            collective_id=0, has_side_effects=True, vmem_limit_bytes=60 * 2 ** 20),
    )(hidden_in, value_weight, queries, keys, level_weights, out_grad)


def solution(mesh):
    return jax.shard_map(
        local,
        mesh=mesh,
        in_specs=(
            P("seq", "head"),
            P(None, "head"),
            P("seq", "head"),
            P("seq", "head"),
            P(None, "head", "seq"),
            P("seq", "head"),
        ),
        out_specs=(P("seq", "head"), P("seq", "head")),
        check_vma=False,
    )
```
